32 devices in a mesh: chaos: 4 (over z), gx: 4 (over y, x), gy: 2 (over core).
Axes of the slice: x: 2, y: 2, z: 4, core: 2. Of those that a mesh axis runs over, the one named last changes fastest.
Arguments:
- lam_start: float32 [286, 16, 512], P(None, ('chaos', 'gy'), 'gx'), may hold values from -6 to 6
- adj_source: float32 [286, 16, 512], P(None, ('chaos', 'gy'), 'gx'), may hold values from -6 to 6
- coef_points: float32 [512, 4, 4, 512], P('chaos', None, 'gy', 'gx'), may hold values from 0.1 to 1
- quad_index: int32 [512, 10], replicated, may hold values from 0 to 3
- mode_index: int32 [286, 10], replicated, may hold values from 0 to 3, as said below
Outputs:
- lam_end: float32 [286, 16, 512], P(None, ('chaos', 'gy'), 'gx')
The draws below stay inside these ranges and needn't reach their ends.
Inputs may be any that keep to these rules, and one draw needn't show every extreme that they name: `mode_index`: each row is a multi-index whose degrees sum to at most 3; each such multi-index of 10 inputs appears exactly once.
All inputs are finite; a program needn't handle non-finite values.
Results may differ from the reference program's by a relative error of at most 0.00011.
Values sent between devices are 32-bit elements; how exact they have to be, the bound alone decides.
A program may use at most 64 MiB of HBM per device.

```python
import math
import jax
import jax.numpy as jnp
import numpy as np
from jax import lax

NINP = 10
P_SIZE = 286
Q = 512
STEPS = 2
NX = 512
NYB = 4
NY = 16
N_CHAOS = 4


def index_list(inputs):
    entries = [[0] * inputs]
    for axis_one in range(inputs):
        degree_row = [0] * inputs
        degree_row[axis_one] += 1
        entries.append(degree_row)
    for axis_one in range(inputs):
        for axis_two in range(axis_one, inputs):
            degree_row = [0] * inputs
            degree_row[axis_one] += 1
            degree_row[axis_two] += 1
            entries.append(degree_row)
    for axis_one in range(inputs):
        for axis_two in range(axis_one, inputs):
            for axis_three in range(axis_two, inputs):
                degree_row = [0] * inputs
                degree_row[axis_one] += 1
                degree_row[axis_two] += 1
                degree_row[axis_three] += 1
                entries.append(degree_row)
    return np.array(entries, dtype=np.int32)


def draw_mode_index(key, part):
    table = jnp.asarray(index_list(NINP), jnp.int32)
    order = jax.random.permutation(key, table.shape[0])
    return table[order]


def place_ends(values, rng, low, largest):
    longest = values.shape.index(max(values.shape))
    spots = []
    for shift in (0, 1):
        where = [jax.random.randint(jax.random.fold_in(rng, axis), (), 0, length) for axis, length in enumerate(values.shape)]
        where[longest] = (where[longest] + shift) % values.shape[longest]
        spots.append(tuple(where))
    return values.at[spots[0]].set(low).at[spots[1]].set(largest)


def block_scale(rng, shape, pieces, low, top_value):
    level, own = 1.0, jax.random.fold_in(rng, 6)
    for axis_at, shards_of in pieces:
        steps = jnp.exp(jax.random.uniform(jax.random.fold_in(own, axis_at), (shards_of,), jnp.float32, low / len(pieces), top_value / len(pieces)))
        level = level * jnp.repeat(steps, shape[axis_at] // shards_of).reshape([-1 if axis == axis_at else 1 for axis in range(len(shape))])
    return level


def bell_draw(own_key, dims, spread, limit, pieces=(), held_as=jnp.bfloat16):
    values = spread * jax.random.normal(own_key, dims, jnp.float32)
    if pieces:
        values = values * block_scale(own_key, dims, pieces, -0.22, 0.18)
    return jnp.clip(values, -limit, limit).astype(held_as)


def setup_inputs(seed: int = 0) -> dict:
    arg_keys = jax.random.split(jax.random.key(seed), 6)
    return {
        "lam_start": bell_draw(arg_keys[0], (P_SIZE, NY, NX), 1.0, 6.0, ((1, 8), (2, 4)), jnp.float32),
        "adj_source": bell_draw(arg_keys[1], (P_SIZE, NY, NX), 1.0, 6.0, ((1, 8), (2, 4)), jnp.float32),
        "coef_points": jnp.clip(jnp.exp(math.log(1.0) - 2.3025851 * jax.random.uniform(arg_keys[2], (Q, N_CHAOS, NYB, NX), jnp.float32) ** block_scale(arg_keys[2], (Q, N_CHAOS, NYB, NX), ((0, 4), (2, 2), (3, 4)), -0.2, 0.2)), 0.1, 1.0),
        "quad_index": place_ends(jax.random.randint(arg_keys[3], (Q, NINP), 0, 4), jax.random.fold_in(arg_keys[3], 1), 0, 3).astype(jnp.int32),
        "mode_index": draw_mode_index(jax.random.fold_in(arg_keys[5], 71), 0),
    }


gauss_nodes = (-2.3344142183389773, -0.7419637843027259, 0.7419637843027259, 2.3344142183389773)
gauss_weights = (0.04587585476806849, 0.4541241452319315, 0.4541241452319315, 0.04587585476806849)
mass_shift = 1.0
relax_rate = 0.2
top_prec = lax.Precision.HIGHEST

def tables(quad_index, mode_index):
    node_vals = jnp.array(gauss_nodes, jnp.float32)
    node_wts = jnp.array(gauss_weights, jnp.float32)
    hermite = jnp.stack([jnp.ones_like(node_vals), node_vals, (node_vals * node_vals - 1.0) / math.sqrt(2.0), (node_vals * node_vals * node_vals - 3.0 * node_vals) / math.sqrt(6.0)], 0)
    levels = jnp.arange(4, dtype=jnp.int32)
    quad_hot = (quad_index[:, :, None] == levels[None, None, :]).astype(jnp.float32)
    mode_hot = (mode_index[:, :, None] == levels[None, None, :]).astype(jnp.float32)
    at_nodes = jnp.einsum('qdk,nk->qdn', quad_hot, hermite, precision=top_prec)
    factors = jnp.einsum('qdn,pdn->qpd', at_nodes, mode_hot, precision=top_prec)
    chaos_basis = jnp.prod(factors, axis=2)
    point_wts = jnp.prod(lax.optimization_barrier(jnp.sum(quad_hot * node_wts[None, None, :], axis=2)), axis=1)
    point_wts = point_wts / jnp.sum(point_wts)
    back_map = chaos_basis * point_wts[:, None]
    return (chaos_basis, back_map)

def operate(current, coef_rows, chaos_basis, back_map):
    padded_y = jnp.pad(current, ((0, 0), (1, 1), (0, 0)))

    def point_flux(row_start):
        slab = lax.dynamic_slice_in_dim(padded_y, row_start, NYB + 2, 1)
        center = slab[:, 1:-1]
        grad_x = (jnp.roll(center, -1, 2) - jnp.roll(center, 1, 2)) * 0.5
        grad_y = (slab[:, 2:] - slab[:, :-2]) * 0.5
        gradients = jnp.stack([grad_x, grad_y], 1)
        at_points = jnp.dot(chaos_basis, gradients.reshape(P_SIZE, -1), precision=top_prec, preferred_element_type=jnp.float32).reshape(Q, 2, NYB, NX)
        coef_block = lax.dynamic_slice_in_dim(coef_rows, row_start, NYB, 1)
        flux_points = at_points * coef_block[:, None]
        return jnp.dot(back_map.T, flux_points.reshape(Q, -1), precision=top_prec, preferred_element_type=jnp.float32).reshape(P_SIZE, 2, NYB, NX)
    starts = jnp.arange(N_CHAOS, dtype=jnp.int32) * NYB
    mapped = lax.map(point_flux, starts)
    fluxes = jnp.transpose(mapped, (1, 2, 0, 3, 4)).reshape(P_SIZE, 2, NY, NX)
    flux_x = fluxes[:, 0]
    flux_yp = jnp.pad(fluxes[:, 1], ((0, 0), (1, 1), (0, 0)))
    divergence = (jnp.roll(flux_x, -1, 2) - jnp.roll(flux_x, 1, 2)) * 0.5 + (flux_yp[:, 2:] - flux_yp[:, :-2]) * 0.5
    return mass_shift * current - divergence

def reference(lam_start, adj_source, coef_points, quad_index, mode_index):
    chaos_basis, back_map = tables(quad_index, mode_index)
    coef_rows = coef_points.reshape(Q, NY, NX)
    lam_now = lam_start
    for repeat in range(STEPS):
        lam_now = lam_now + relax_rate * (adj_source - operate(lam_now, coef_rows, chaos_basis, back_map))
    return lam_now
```

```python
import math

import jax
import jax.numpy as jnp
from jax import lax
from jax.sharding import PartitionSpec as P

STEPS = 2


gauss_nodes = (-2.3344142183389773, -0.7419637843027259, 0.7419637843027259, 2.3344142183389773)
gauss_weights = (0.04587585476806849, 0.4541241452319315, 0.4541241452319315, 0.04587585476806849)
mass_shift = 1.0
relax_rate = 0.2
top_prec = lax.Precision.HIGHEST


def tables(quad_index, mode_index):
    node_vals = jnp.array(gauss_nodes, jnp.float32)
    node_wts = jnp.array(gauss_weights, jnp.float32)
    hermite = jnp.stack(
        [
            jnp.ones_like(node_vals),
            node_vals,
            (node_vals * node_vals - 1.0) / math.sqrt(2.0),
            (node_vals * node_vals * node_vals - 3.0 * node_vals) / math.sqrt(6.0),
        ],
        0,
    )
    levels = jnp.arange(4, dtype=jnp.int32)
    quad_hot = (quad_index[:, :, None] == levels[None, None, :]).astype(jnp.float32)
    mode_hot = (mode_index[:, :, None] == levels[None, None, :]).astype(jnp.float32)
    at_nodes = jnp.einsum("qdk,nk->qdn", quad_hot, hermite, precision=top_prec)
    factors = jnp.einsum("qdn,pdn->qpd", at_nodes, mode_hot, precision=top_prec)
    chaos_basis = jnp.prod(factors, axis=2)
    point_wts = jnp.prod(jnp.sum(quad_hot * node_wts[None, None, :], axis=2), axis=1)
    point_wts = point_wts / jnp.sum(point_wts)
    back_map = chaos_basis * point_wts[:, None]
    return (chaos_basis, back_map)


def shift_pair(low, high, axis):
    size = lax.axis_size(axis)
    up = [(i, (i + 1) % size) for i in range(size)]
    down = [(j, i) for i, j in up]
    return lax.ppermute(high, axis, up), lax.ppermute(low, axis, down)


def local(lam_start, adj_source, coef_points, quad_index, mode_index):
    modes, row_len, col_len = lam_start.shape
    points = quad_index.shape[0]
    rows = ("chaos", "gy")
    row_dev = lax.axis_index(rows)
    row_devs = lax.axis_size(rows)
    keep_low = jnp.where(row_dev == 0, 0.0, 1.0).astype(jnp.float32)
    keep_high = jnp.where(row_dev == row_devs - 1, 0.0, 1.0).astype(jnp.float32)
    coef = lax.all_to_all(coef_points, "chaos", split_axis=1, concat_axis=0, tiled=True)
    coef = coef.reshape(points, row_len, col_len)
    k_low, k_high = shift_pair(coef[:, 0], coef[:, -1], rows)
    k_left, k_right = shift_pair(coef[:, :, :1], coef[:, :, -1:], "gx")
    chaos_basis, back_map = tables(quad_index, mode_index)
    coef_y = [k_low * keep_low] + [coef[:, r] for r in range(row_len)] + [k_high * keep_high]
    coef_x = [jnp.concatenate([k_left[:, r], coef[:, r], k_right[:, r]], 1) for r in range(row_len)]
    lam_now = lam_start
    for repeat in range(STEPS):
        v_low, v_high = shift_pair(lam_now[:, :2], lam_now[:, -2:], rows)
        v_left, v_right = shift_pair(lam_now[:, :, :2], lam_now[:, :, -2:], "gx")
        v_low = v_low * keep_low
        v_high = v_high * keep_high
        parts = [v_low[:, 0], v_low[:, 1]] + [lam_now[:, r] for r in range(row_len)] + [v_high[:, 0], v_high[:, 1]]
        edges = [v_left[:, r] for r in range(row_len)] + [v_right[:, r] for r in range(row_len)]
        u = jnp.dot(chaos_basis, jnp.concatenate(parts + edges, 1), precision=top_prec, preferred_element_type=jnp.float32)
        u_row = [u[:, i * col_len : (i + 1) * col_len] for i in range(row_len + 4)]
        base = (row_len + 4) * col_len
        u_left = [u[:, base + 2 * r : base + 2 * r + 2] for r in range(row_len)]
        base += 2 * row_len
        u_right = [u[:, base + 2 * r : base + 2 * r + 2] for r in range(row_len)]
        flux_y = [coef_y[i] * ((u_row[i + 2] - u_row[i]) * 0.5) for i in range(row_len + 2)]
        div = []
        for r in range(row_len):
            wide = jnp.concatenate([u_left[r], u_row[r + 2], u_right[r]], 1)
            flux_x = coef_x[r] * ((wide[:, 2:] - wide[:, :-2]) * 0.5)
            div.append((flux_x[:, 2:] - flux_x[:, :-2]) * 0.5 + (flux_y[r + 2] - flux_y[r]) * 0.5)
        back = jnp.dot(back_map.T, jnp.concatenate(div, 1), precision=top_prec, preferred_element_type=jnp.float32)
        divergence = back.reshape(modes, row_len, col_len)
        lam_now = lam_now + relax_rate * (adj_source - (mass_shift * lam_now - divergence))
    return lam_now


def solution(mesh):
    placed = (
        P(None, ("chaos", "gy"), "gx"),
        P(None, ("chaos", "gy"), "gx"),
        P("chaos", None, "gy", "gx"),
        P(),
        P(),
    )
    return jax.shard_map(
        local, mesh=mesh, in_specs=placed, out_specs=P(None, ("chaos", "gy"), "gx"), check_vma=False
    )
```

```python
import functools
import math

import jax
import jax.numpy as jnp
from jax import lax
from jax.experimental import pallas as pl
from jax.experimental.pallas import tpu as pltpu
from jax.sharding import PartitionSpec as P

STEPS = 2
SUB = 32

gauss_nodes = (-2.3344142183389773, -0.7419637843027259, 0.7419637843027259, 2.3344142183389773)
gauss_weights = (0.04587585476806849, 0.4541241452319315, 0.4541241452319315, 0.04587585476806849)
mass_shift = 1.0
relax_rate = 0.2
f32 = jnp.float32
bf16 = jnp.bfloat16


def split(x):
    high = x.astype(bf16)
    return high, (x - high.astype(f32)).astype(bf16)


def dot3(ah, al, bh, bl):
    dot = functools.partial(jnp.dot, preferred_element_type=f32)
    return dot(ah, bh) + (dot(ah, bl) + dot(al, bh))


def kernel(
    dims, lam_ref, adj_ref, coef_ref, quad_ref, mode_ref, out_ref,
    kfull, kedge, ksend, krecv, vhalo, vsend, vrecv, lam1, u,
    psi, psi_h, psi_l, bt_h, bt_l, d_h, d_l,
    main_send, main_recv, fwd_send, fwd_recv, v_send, v_recv,
):
    n, ncore, ngx, inputs, modes, rows_p, wide, points, pts = dims
    z, x, c = lax.axis_index("chaos"), lax.axis_index("gx"), lax.axis_index("gy")
    count = n * ncore
    me = z * ncore + c
    above = lax.rem(me + 1, count)
    below = lax.rem(me + count - 1, count)
    has_above, has_below = me < count - 1, me > 0
    dev_above = {"chaos": lax.div(above, ncore), "gy": lax.rem(above, ncore)}
    dev_below = {"chaos": lax.div(below, ncore), "gy": lax.rem(below, ncore)}
    dev_right = {"gx": lax.rem(x + 1, ngx)}
    dev_left = {"gx": lax.rem(x + ngx - 1, ngx)}

    def remote(src, dst, ss, rs, dev):
        return pltpu.make_async_remote_copy(
            src_ref=src, dst_ref=dst, send_sem=ss, recv_sem=rs, device_id=dev,
            device_id_type=pl.DeviceIdType.MESH,
        )

    barrier = pltpu.get_barrier_semaphore()

    def greet(dev):
        pl.semaphore_signal(barrier, inc=1, device_id=dev, device_id_type=pl.DeviceIdType.MESH)

    for d in range(1, n):
        greet({"chaos": lax.rem(z + d, n)})
    greet(dev_left)
    greet(dev_right)

    greet(dev_above)
    greet(dev_below)
    pl.semaphore_wait(barrier, n + 3)

    def main_copy(to):
        return remote(coef_ref.at[to], kfull.at[z, pl.ds(1, 2)], main_send.at[to], main_recv.at[z], {"chaos": to})

    def v_copies(step, src):
        return (
            remote(src, vhalo.at[step, 0], v_send.at[step, 0], v_recv.at[step, 0], dev_above),
            remote(src, vhalo.at[step, 1], v_send.at[step, 1], v_recv.at[step, 1], dev_below),
            remote(vsend.at[step, 0], vrecv.at[step, 1], v_send.at[step, 2], v_recv.at[step, 2], dev_left),
            remote(vsend.at[step, 1], vrecv.at[step, 0], v_send.at[step, 3], v_recv.at[step, 3], dev_right),
        )

    def start_v(step, src):
        up, down, left, right = v_copies(step, src)

        @pl.when(has_above)
        def _():
            up.start()

        @pl.when(has_below)
        def _():
            down.start()

        for r in range(2):
            flipped = jnp.concatenate([src[r], jnp.zeros((wide - rows_p, 128), f32)], 0).T
            vsend[step, 0, r] = flipped[:8]
            vsend[step, 1, r] = flipped[120:]
        left.start()
        right.start()

    def fwd_copies(j):
        return (
            remote(kfull.at[j, 2], kfull.at[j, 0], fwd_send.at[0, j], fwd_recv.at[0, j], dev_above),
            remote(kfull.at[j, 1], kfull.at[j, 3], fwd_send.at[1, j], fwd_recv.at[1, j], dev_below),
            remote(ksend.at[j, 0], krecv.at[j, 1], fwd_send.at[2, j], fwd_recv.at[2, j], dev_left),
            remote(ksend.at[j, 1], krecv.at[j, 0], fwd_send.at[3, j], fwd_recv.at[3, j], dev_right),
        )

    def forward(j):
        up, down, left, right = fwd_copies(j)

        @pl.when(has_above)
        def _():
            up.start()

        @pl.when(has_below)
        def _():
            down.start()

        for r in range(2):
            flipped = kfull[j, 1 + r].T
            ksend[j, 0, r] = flipped[:8]
            ksend[j, 1, r] = flipped[120:]
        left.start()
        right.start()

    for d in range(1, n):
        main_copy(lax.rem(z + d, n)).start()
    start_v(0, lam_ref)
    kfull[z, pl.ds(1, 2)] = coef_ref[z]
    forward(z)

    @pl.when(jnp.logical_not(has_below))
    def _():
        kfull[:, 0] = jnp.zeros((n, pts, 128), f32)
        vhalo[:, 0] = jnp.zeros((STEPS, 2, rows_p, 128), f32)

    @pl.when(jnp.logical_not(has_above))
    def _():
        kfull[:, 3] = jnp.zeros((n, pts, 128), f32)
        vhalo[:, 1] = jnp.zeros((STEPS, 2, rows_p, 128), f32)

    lane = lax.broadcasted_iota(jnp.int32, (1, 128), 1)
    quad = quad_ref[...]
    wts = jnp.where((quad == 0) | (quad == 3), gauss_weights[0], gauss_weights[1]).astype(f32)
    wts = jnp.where(lane < inputs, wts, 1.0)
    shift = 8
    while shift:
        wts = wts * pltpu.roll(wts, 128 - shift, 1)
        shift //= 2
    wts = wts[:, :1]
    wts = wts / jnp.sum(wts, axis=0, keepdims=True) * 0.25
    keep = jnp.where(lax.broadcasted_iota(jnp.int32, (SUB, wide), 1) < modes, 1.0, 0.0).astype(f32)

    def basis(i, carry):
        rows = pl.ds(pl.multiple_of(i * SUB, SUB), SUB)
        q = quad_ref[rows, :]
        node = jnp.where(
            q == 0, gauss_nodes[0], jnp.where(q == 1, gauss_nodes[1], jnp.where(q == 2, gauss_nodes[2], gauss_nodes[3]))
        ).astype(f32)
        h2 = (node * node - 1.0) * (1.0 / math.sqrt(2.0))
        h3 = (node * node * node - 3.0 * node) * (1.0 / math.sqrt(6.0))
        total = keep
        for d in range(inputs):
            deg = mode_ref[d : d + 1, :]
            total = total * jnp.where(
                deg == 0,
                1.0,
                jnp.where(deg == 1, node[:, d : d + 1], jnp.where(deg == 2, h2[:, d : d + 1], h3[:, d : d + 1])),
            )
        psi[rows, :] = total
        high, low = split(total)
        psi_h[rows, :] = high
        psi_l[rows, :] = low
        return carry

    lax.fori_loop(0, points // SUB, basis, 0)
    for i in range(points // 128):
        part = slice(i * 128, i * 128 + 128)
        flipped = (psi[part, :] * wts[part]).T[:rows_p]
        high, low = split(flipped)
        bt_h[:, part] = high
        bt_l[:, part] = low

    def to_points(at, first, second):
        vh, vl = split(jnp.concatenate([first, second], 1))
        res = dot3(psi_h[:, :rows_p], psi_l[:, :rows_p], vh, vl)
        u[at] = res[:, :128]
        u[at + 1] = res[:, 128:]

    def fields(step, src):
        to_points(2, src[0], src[1])
        up, down, left, right = v_copies(step, src)

        @pl.when(has_below)
        def _():
            up.wait_recv()

        to_points(0, vhalo[step, 0, 0], vhalo[step, 0, 1])

        @pl.when(has_above)
        def _():
            down.wait_recv()

        to_points(4, vhalo[step, 1, 0], vhalo[step, 1, 1])
        left.wait_recv()
        right.wait_recv()
        edge = [
            jnp.concatenate([vrecv[step, 1, r], jnp.zeros((112, wide), f32), vrecv[step, 0, r]], 0).T[:rows_p]
            for r in range(2)
        ]
        to_points(6, edge[0], edge[1])

    is_first, is_last = lane == 0, lane == 127

    def stencil(i, carry):
        rows = pl.ds(pl.multiple_of(i * SUB, SUB), SUB)
        per = pts // SUB
        j = lax.div(i, per)
        sub = pl.ds(pl.multiple_of(lax.rem(i, per) * SUB, SUB), SUB)
        uy = [u[k, rows, :] for k in range(8)]
        ky = [kfull[j, k, sub, :] for k in range(4)]
        fy = [ky[k] * (uy[k + 2] - uy[k]) for k in range(4)]
        for r in range(2):
            mid, end = uy[2 + r], uy[6 + r]
            a, b = pltpu.roll(mid, 127, 1), pltpu.roll(end, 127, 1)
            e, f = pltpu.roll(mid, 1, 1), pltpu.roll(end, 1, 1)
            fx = ky[1 + r] * (jnp.where(is_last, b, a) - jnp.where(is_first, f, e))
            fe = kedge[j, r, sub, :] * (jnp.where(is_last, a, b) - jnp.where(is_first, e, f))
            nxt = jnp.where(is_last, pltpu.roll(fe, 127, 1), pltpu.roll(fx, 127, 1))
            prv = jnp.where(is_first, pltpu.roll(fe, 1, 1), pltpu.roll(fx, 1, 1))
            high, low = split((nxt - prv) + (fy[r + 2] - fy[r]))
            d_h[rows, r * 128 : r * 128 + 128] = high
            d_l[rows, r * 128 : r * 128 + 128] = low
        return carry

    def update(src, dst):
        lax.fori_loop(0, points // SUB, stencil, 0)
        div = dot3(bt_h[...], bt_l[...], d_h[...], d_l[...])
        for r in range(2):
            v = src[r]
            dst[r] = v + relax_rate * (adj_ref[r] - (mass_shift * v - div[:, r * 128 : r * 128 + 128]))

    for d in range(1, n):
        j = lax.rem(z + d, n)
        remote(coef_ref.at[j], kfull.at[j, pl.ds(1, 2)], main_send.at[j], main_recv.at[j], {"chaos": j}).wait_recv()
        forward(j)
    fields(0, lam_ref)

    def arrive(j, carry):
        up, down, left, right = fwd_copies(j)

        @pl.when(has_below)
        def _():
            up.wait_recv()

        @pl.when(has_above)
        def _():
            down.wait_recv()

        left.wait_recv()
        right.wait_recv()
        for r in range(2):
            kedge[j, r] = jnp.concatenate([krecv[j, 1, r], jnp.zeros((112, pts), f32), krecv[j, 0, r]], 0).T
        return carry

    lax.fori_loop(0, n, arrive, 0)
    update(lam_ref, lam1)
    start_v(1, lam1)
    fields(1, lam1)
    update(lam1, out_ref)

    for d in range(1, n):
        main_copy(lax.rem(z + d, n)).wait_send()

    def drain(copies):
        up, down, left, right = copies

        @pl.when(has_above)
        def _():
            up.wait_send()

        @pl.when(has_below)
        def _():
            down.wait_send()

        left.wait_send()
        right.wait_send()

    def drain_one(j, carry):
        drain(fwd_copies(j))
        return carry

    lax.fori_loop(0, n, drain_one, 0)
    drain(v_copies(0, lam_ref))
    drain(v_copies(1, lam1))


def local(mesh_sizes, lam_start, adj_source, coef_points, quad_index, mode_index):
    n, ngx, ncore = mesh_sizes
    modes = lam_start.shape[0]
    points, inputs = quad_index.shape
    pts = coef_points.shape[0]
    rows_p = -(-modes // 16) * 16
    wide = -(-modes // 128) * 128
    dims = (n, ncore, ngx, inputs, modes, rows_p, wide, points, pts)

    def by_row(v):
        return jnp.pad(jnp.transpose(v, (1, 0, 2)), ((0, 0), (0, rows_p - modes), (0, 0)))

    coef = jnp.transpose(coef_points, (1, 2, 0, 3))
    quad = jnp.pad(quad_index, ((0, 0), (0, 128 - inputs)))
    mode = jnp.pad(mode_index.T, ((0, 16 - inputs), (0, wide - modes)))
    vmem = pl.BlockSpec(memory_space=pltpu.VMEM)
    dma = pltpu.SemaphoreType.DMA
    out = pl.pallas_call(
        functools.partial(kernel, dims),
        out_shape=jax.ShapeDtypeStruct((2, rows_p, 128), f32),
        in_specs=[vmem] * 5,
        out_specs=vmem,
        scratch_shapes=[
            pltpu.VMEM((n, 4, pts, 128), f32),
            pltpu.VMEM((n, 2, pts, 128), f32),
            pltpu.VMEM((n, 2, 2, 8, pts), f32),
            pltpu.VMEM((n, 2, 2, 8, pts), f32),
            pltpu.VMEM((STEPS, 2, 2, rows_p, 128), f32),
            pltpu.VMEM((STEPS, 2, 2, 8, wide), f32),
            pltpu.VMEM((STEPS, 2, 2, 8, wide), f32),
            pltpu.VMEM((2, rows_p, 128), f32),
            pltpu.VMEM((8, points, 128), f32),
            pltpu.VMEM((points, wide), f32),
            pltpu.VMEM((points, wide), bf16),
            pltpu.VMEM((points, wide), bf16),
            pltpu.VMEM((rows_p, points), bf16),
            pltpu.VMEM((rows_p, points), bf16),
            pltpu.VMEM((points, 256), bf16),
            pltpu.VMEM((points, 256), bf16),
            dma((n,)), dma((n,)), dma((4, n)), dma((4, n)), dma((STEPS, 4)), dma((STEPS, 4)),
        ],
        compiler_params=pltpu.CompilerParams(
            collective_id=0, has_side_effects=True, vmem_limit_bytes=40 * 1024 * 1024
        ),
    )(by_row(lam_start), by_row(adj_source), coef, quad, mode)
    return jnp.transpose(out[:, :modes], (1, 0, 2))


def solution(mesh):
    sizes = (mesh.shape["chaos"], mesh.shape["gx"], mesh.shape["gy"])
    placed = (
        P(None, ("chaos", "gy"), "gx"),
        P(None, ("chaos", "gy"), "gx"),
        P("chaos", None, "gy", "gx"),
        P(),
        P(),
    )
    return jax.shard_map(
        functools.partial(local, sizes),
        mesh=mesh,
        in_specs=placed,
        out_specs=P(None, ("chaos", "gy"), "gx"),
        check_vma=False,
    )
```

```python
import functools
import math

import jax
import jax.numpy as jnp
from jax import lax
from jax.experimental import pallas as pl
from jax.experimental.pallas import tpu as pltpu
from jax.sharding import PartitionSpec as P

STEPS = 2
SUB = 32
TILE = 128

gauss_nodes = (-2.3344142183389773, -0.7419637843027259, 0.7419637843027259, 2.3344142183389773)
gauss_weights = (0.04587585476806849, 0.4541241452319315, 0.4541241452319315, 0.04587585476806849)
mass_shift = 1.0
relax_rate = 0.2
f32 = jnp.float32
bf16 = jnp.bfloat16


def split(x):
    high = x.astype(bf16)
    return high, (x - high.astype(f32)).astype(bf16)


def dot3(ah, al, bh, bl):
    dot = functools.partial(jnp.dot, preferred_element_type=f32)
    return dot(ah, bh) + (dot(ah, bl) + dot(al, bh))


def kernel(
    dims, lam_raw, adj_hbm, coef_ref, quad_ref, mode_raw, out_ref,
    adj_ref, in_sem, lam_ref, mode_ref,    kfull, kedge, ksend, krecv, vhalo, vsend, vrecv, lam1, u,
    psi, psi_h, psi_l, bt_h, bt_l, d_h, d_l, d_x,
    main_send, main_recv, fwd_send, fwd_recv, v_send, v_recv,
):
    n, ncore, ngx, inputs, modes, rows_p, wide, points, pts = dims
    z, x, c = lax.axis_index("chaos"), lax.axis_index("gx"), lax.axis_index("gy")
    count = n * ncore
    me = z * ncore + c
    above = lax.rem(me + 1, count)
    below = lax.rem(me + count - 1, count)
    has_above, has_below = me < count - 1, me > 0
    dev_above = {"chaos": lax.div(above, ncore), "gy": lax.rem(above, ncore)}
    dev_below = {"chaos": lax.div(below, ncore), "gy": lax.rem(below, ncore)}
    dev_right = {"gx": lax.rem(x + 1, ngx)}
    dev_left = {"gx": lax.rem(x + ngx - 1, ngx)}

    def remote(src, dst, ss, rs, dev):
        return pltpu.make_async_remote_copy(
            src_ref=src, dst_ref=dst, send_sem=ss, recv_sem=rs, device_id=dev,
            device_id_type=pl.DeviceIdType.MESH,
        )

    fetch = pltpu.make_async_copy(adj_hbm, adj_ref, in_sem)
    fetch.start()
    barrier = pltpu.get_barrier_semaphore()

    def greet(dev):
        pl.semaphore_signal(barrier, inc=1, device_id=dev, device_id_type=pl.DeviceIdType.MESH)

    for d in range(1, n):
        greet({"chaos": lax.rem(z + d, n)})
    greet(dev_left)
    greet(dev_right)

    greet(dev_above)
    greet(dev_below)
    pl.semaphore_wait(barrier, n + 3)

    def main_copy(to):
        return remote(coef_ref.at[to], kfull.at[z, pl.ds(1, 2)], main_send.at[to], main_recv.at[z], {"chaos": to})

    def v_copies(step, src):
        return (
            remote(src, vhalo.at[step, 0], v_send.at[step, 0], v_recv.at[step, 0], dev_above),
            remote(src, vhalo.at[step, 1], v_send.at[step, 1], v_recv.at[step, 1], dev_below),
            remote(vsend.at[step, 0], vrecv.at[step, 1], v_send.at[step, 2], v_recv.at[step, 2], dev_left),
            remote(vsend.at[step, 1], vrecv.at[step, 0], v_send.at[step, 3], v_recv.at[step, 3], dev_right),
        )

    def start_v(step, src):
        up, down, left, right = v_copies(step, src)

        @pl.when(has_above)
        def _():
            up.start()

        @pl.when(has_below)
        def _():
            down.start()

        for r in range(2):
            flipped = jnp.concatenate([src[r], jnp.zeros((wide - rows_p, 128), f32)], 0).T
            vsend[step, 0, r] = flipped[:8]
            vsend[step, 1, r] = flipped[120:]
        left.start()
        right.start()

    def fwd_copies(j):
        return (
            remote(kfull.at[j, 2], kfull.at[j, 0], fwd_send.at[0, j], fwd_recv.at[0, j], dev_above),
            remote(kfull.at[j, 1], kfull.at[j, 3], fwd_send.at[1, j], fwd_recv.at[1, j], dev_below),
            remote(ksend.at[j, 0], krecv.at[j, 1], fwd_send.at[2, j], fwd_recv.at[2, j], dev_left),
            remote(ksend.at[j, 1], krecv.at[j, 0], fwd_send.at[3, j], fwd_recv.at[3, j], dev_right),
        )

    def forward(j):
        up, down, left, right = fwd_copies(j)

        @pl.when(has_above)
        def _():
            up.start()

        @pl.when(has_below)
        def _():
            down.start()

        for r in range(2):
            flipped = kfull[j, 1 + r].T
            ksend[j, 0, r] = flipped[:8]
            ksend[j, 1, r] = flipped[120:]
        left.start()
        right.start()

    for d in range(1, n):
        main_copy(lax.rem(z + d, n)).start()
    for r in range(2):
        lam_ref[r, :modes] = lam_raw[:, r, :]
        lam_ref[r, modes:] = jnp.zeros((rows_p - modes, 128), f32)
    start_v(0, lam_ref)
    kfull[z, pl.ds(1, 2)] = coef_ref[z]
    forward(z)

    @pl.when(jnp.logical_not(has_below))
    def _():
        kfull[:, 0] = jnp.zeros((n, pts, 128), f32)
        vhalo[:, 0] = jnp.zeros((STEPS, 2, rows_p, 128), f32)

    @pl.when(jnp.logical_not(has_above))
    def _():
        kfull[:, 3] = jnp.zeros((n, pts, 128), f32)
        vhalo[:, 1] = jnp.zeros((STEPS, 2, rows_p, 128), f32)

    lane = lax.broadcasted_iota(jnp.int32, (1, 128), 1)
    quad = quad_ref[...]
    each = jnp.where((quad == 0) | (quad == 3), gauss_weights[0], gauss_weights[1]).astype(f32)
    wts = each[:, :1]
    for d in range(1, inputs):
        wts = wts * each[:, d : d + 1]
    mode_ref[...] = jnp.zeros((16, wide), f32)
    mode_ref[:inputs, :modes] = mode_raw[...].astype(f32)
    wts = wts / jnp.sum(wts, axis=0, keepdims=True) * 0.25
    keep = jnp.where(lax.broadcasted_iota(jnp.int32, (SUB, wide), 1) < modes, 1.0, 0.0).astype(f32)

    def basis(i, carry):
        rows = pl.ds(pl.multiple_of(i * SUB, SUB), SUB)
        q = quad_ref[rows, :]
        node = jnp.where(
            q == 0, gauss_nodes[0], jnp.where(q == 1, gauss_nodes[1], jnp.where(q == 2, gauss_nodes[2], gauss_nodes[3]))
        ).astype(f32)
        h2 = (node * node - 1.0) * (1.0 / math.sqrt(2.0))
        h3 = (node * node * node - 3.0 * node) * (1.0 / math.sqrt(6.0))
        total = keep
        for d in range(inputs):
            deg = mode_ref[d : d + 1, :]
            total = total * jnp.where(
                deg == 0.0,
                1.0,
                jnp.where(deg == 1.0, node[:, d : d + 1], jnp.where(deg == 2.0, h2[:, d : d + 1], h3[:, d : d + 1])),
            )
        psi[rows, :] = total
        high, low = split(total)
        psi_h[rows, :] = high
        psi_l[rows, :] = low
        return carry

    lax.fori_loop(0, points // SUB, basis, 0)
    for i in range(points // 128):
        part = slice(i * 128, i * 128 + 128)
        flipped = (psi[part, :] * wts[part]).T[:rows_p]
        high, low = split(flipped)
        bt_h[:, part] = high
        bt_l[:, part] = low

    def to_points(at, first, second):
        vh, vl = split(jnp.concatenate([first, second], 1))
        res = dot3(psi_h[:, :rows_p], psi_l[:, :rows_p], vh, vl)
        u[at] = res[:, :128]
        u[at + 1] = res[:, 128:]

    def own(src):
        to_points(2, src[0], src[1])

    def sides(step, src):
        left, right = v_copies(step, src)[2:]
        left.wait_recv()
        right.wait_recv()
        edge = [
            jnp.concatenate([vrecv[step, 1, r], jnp.zeros((112, wide), f32), vrecv[step, 0, r]], 0).T[:rows_p]
            for r in range(2)
        ]
        to_points(6, edge[0], edge[1])

    def halo_rows(step, src):
        up, down = v_copies(step, src)[:2]

        @pl.when(has_below)
        def _():
            up.wait_recv()

        to_points(0, vhalo[step, 0, 0], vhalo[step, 0, 1])

        @pl.when(has_above)
        def _():
            down.wait_recv()

        to_points(4, vhalo[step, 1, 0], vhalo[step, 1, 1])

    is_first, is_last = lane == 0, lane == 127

    tile = min(pts, TILE)

    def across(j, i):
        rows = pl.ds(pl.multiple_of(j * pts + i * tile, tile), tile)
        sub = pl.ds(i * tile, tile)
        for r in range(2):
            mid, end = u[2 + r, rows, :], u[6 + r, rows, :]
            a, b = pltpu.roll(mid, 127, 1), pltpu.roll(end, 127, 1)
            e, f = pltpu.roll(mid, 1, 1), pltpu.roll(end, 1, 1)
            fx = kfull[j, 1 + r, sub, :] * (jnp.where(is_last, b, a) - jnp.where(is_first, f, e))
            fe = kedge[j, r, sub, :] * (jnp.where(is_last, a, b) - jnp.where(is_first, e, f))
            nxt = jnp.where(is_last, pltpu.roll(fe, 127, 1), pltpu.roll(fx, 127, 1))
            prv = jnp.where(is_first, pltpu.roll(fe, 1, 1), pltpu.roll(fx, 1, 1))
            d_x[r, rows, :] = nxt - prv

    def along(j, i):
        rows = pl.ds(pl.multiple_of(j * pts + i * tile, tile), tile)
        sub = pl.ds(i * tile, tile)
        uy = [u[k, rows, :] for k in range(6)]
        fy = [kfull[j, k, sub, :] * (uy[k + 2] - uy[k]) for k in range(4)]
        for r in range(2):
            high, low = split(d_x[r, rows, :] + (fy[r + 2] - fy[r]))
            d_h[rows, r * 128 : r * 128 + 128] = high
            d_l[rows, r * 128 : r * 128 + 128] = low

    def chunk(part, j):
        for i in range(pts // tile):
            part(j, i)

    def update(src, store):
        div = dot3(bt_h[...], bt_l[...], d_h[...], d_l[...])
        for r in range(2):
            v = src[r, :modes]
            store(r, v + relax_rate * (adj_ref[:, r, :] - (mass_shift * v - div[:modes, r * 128 : r * 128 + 128])))

    def receive(d):
        j = lax.rem(z + n - d, n)
        remote(coef_ref.at[j], kfull.at[j, pl.ds(1, 2)], main_send.at[j], main_recv.at[j], {"chaos": j}).wait_recv()
        forward(j)

    receive(1)
    third = n // 2

    own(lam_ref)
    for d in range(2, third + 1):
        receive(d)
    sides(0, lam_ref)
    halo_rows(0, lam_ref)
    for d in range(max(2, third + 1), n):
        receive(d)

    def arrive(d, carry):
        j = lax.rem(z + n - d, n)
        up, down, left, right = fwd_copies(j)
        left.wait_recv()
        right.wait_recv()
        for r in range(2):
            kedge[j, r] = jnp.concatenate([krecv[j, 1, r], jnp.zeros((112, pts), f32), krecv[j, 0, r]], 0).T
        chunk(across, j)

        @pl.when(has_below)
        def _():
            up.wait_recv()

        @pl.when(has_above)
        def _():
            down.wait_recv()

        chunk(along, j)
        return carry

    lax.fori_loop(0, n, arrive, 0)

    def keep_lam(r, value):
        lam1[r, :modes] = value
        lam1[r, modes:] = jnp.zeros((rows_p - modes, 128), f32)

    def give(r, value):
        out_ref[:, r, :] = value

    fetch.wait()
    update(lam_ref, keep_lam)
    start_v(1, lam1)
    own(lam1)
    sides(1, lam1)

    def wide_again(j, carry):
        chunk(across, j)
        return carry

    def tall_again(j, carry):
        chunk(along, j)
        return carry

    lax.fori_loop(0, n, wide_again, 0)
    halo_rows(1, lam1)
    lax.fori_loop(0, n, tall_again, 0)
    update(lam1, give)

    for d in range(1, n):
        main_copy(lax.rem(z + d, n)).wait_send()

    def drain(copies):
        up, down, left, right = copies

        @pl.when(has_above)
        def _():
            up.wait_send()

        @pl.when(has_below)
        def _():
            down.wait_send()

        left.wait_send()
        right.wait_send()

    def drain_one(j, carry):
        drain(fwd_copies(j))
        return carry

    lax.fori_loop(0, n, drain_one, 0)
    drain(v_copies(0, lam_ref))
    drain(v_copies(1, lam1))


def local(mesh_sizes, lam_start, adj_source, coef_points, quad_index, mode_index):
    n, ngx, ncore = mesh_sizes
    modes = lam_start.shape[0]
    points, inputs = quad_index.shape
    pts = coef_points.shape[0]
    rows_p = -(-modes // 16) * 16
    wide = -(-modes // 128) * 128
    dims = (n, ncore, ngx, inputs, modes, rows_p, wide, points, pts)

    vmem = pl.BlockSpec(memory_space=pltpu.VMEM)
    dma = pltpu.SemaphoreType.DMA
    out = pl.pallas_call(
        functools.partial(kernel, dims),
        out_shape=jax.ShapeDtypeStruct((modes, 2, 128), f32),
        in_specs=[vmem, pl.BlockSpec(memory_space=pltpu.HBM), vmem, vmem, vmem],
        out_specs=vmem,
        scratch_shapes=[
            pltpu.VMEM(lam_start.shape, f32),
            pltpu.SemaphoreType.DMA,
            pltpu.VMEM((2, rows_p, 128), f32),
            pltpu.VMEM((16, wide), f32),
            pltpu.VMEM((n, 4, pts, 128), f32),
            pltpu.VMEM((n, 2, pts, 128), f32),
            pltpu.VMEM((n, 2, 2, 8, pts), f32),
            pltpu.VMEM((n, 2, 2, 8, pts), f32),
            pltpu.VMEM((STEPS, 2, 2, rows_p, 128), f32),
            pltpu.VMEM((STEPS, 2, 2, 8, wide), f32),
            pltpu.VMEM((STEPS, 2, 2, 8, wide), f32),
            pltpu.VMEM((2, rows_p, 128), f32),
            pltpu.VMEM((8, points, 128), f32),
            pltpu.VMEM((points, wide), f32),
            pltpu.VMEM((points, wide), bf16),
            pltpu.VMEM((points, wide), bf16),
            pltpu.VMEM((rows_p, points), bf16),
            pltpu.VMEM((rows_p, points), bf16),
            pltpu.VMEM((points, 256), bf16),
            pltpu.VMEM((points, 256), bf16),
            pltpu.VMEM((2, points, 128), f32),
            dma((n,)), dma((n,)), dma((4, n)), dma((4, n)), dma((STEPS, 4)), dma((STEPS, 4)),
        ],
        compiler_params=pltpu.CompilerParams(
            collective_id=0, has_side_effects=True, vmem_limit_bytes=40 * 1024 * 1024
        ),
    )(lam_start, adj_source, jnp.transpose(coef_points, (1, 2, 0, 3)), quad_index, mode_index.T)
    return out


def solution(mesh):
    sizes = (mesh.shape["chaos"], mesh.shape["gx"], mesh.shape["gy"])
    placed = (
        P(None, ("chaos", "gy"), "gx"),
        P(None, ("chaos", "gy"), "gx"),
        P("chaos", None, "gy", "gx"),
        P(),
        P(),
    )
    return jax.shard_map(
        functools.partial(local, sizes),
        mesh=mesh,
        in_specs=placed,
        out_specs=P(None, ("chaos", "gy"), "gx"),
        check_vma=False,
    )
```

```python
import functools
import math

import jax
import jax.numpy as jnp
from jax import lax
from jax.experimental import pallas as pl
from jax.experimental.pallas import tpu as pltpu
from jax.sharding import PartitionSpec as P

STEPS = 2
SUB = 32
TILE = 128

gauss_nodes = (-2.3344142183389773, -0.7419637843027259, 0.7419637843027259, 2.3344142183389773)
gauss_weights = (0.04587585476806849, 0.4541241452319315, 0.4541241452319315, 0.04587585476806849)
mass_shift = 1.0
relax_rate = 0.2
f32 = jnp.float32
bf16 = jnp.bfloat16


def split(x):
    high = x.astype(bf16)
    return high, (x - high.astype(f32)).astype(bf16)


def dot3(ah, al, bh, bl):
    dot = functools.partial(jnp.dot, preferred_element_type=f32)
    return dot(ah, bh) + (dot(ah, bl) + dot(al, bh))


def kernel(
    dims, lam_raw, adj_hbm, coef_ref, quad_ref, mode_raw, out_ref,
    adj_ref, in_sem, lam_ref, mode_ref,    kfull, kedge, ksend, krecv, vhalo, vsend, vrecv, lam1, u,
    psi, psi_h, psi_l, bt_h, bt_l, d_h, d_l, d_x,
    main_send, main_recv, fwd_send, fwd_recv, v_send, v_recv,
):
    n, ncore, ngx, inputs, modes, rows_p, wide, points, pts = dims
    z, x, c = lax.axis_index("chaos"), lax.axis_index("gx"), lax.axis_index("gy")
    count = n * ncore
    me = z * ncore + c
    above = lax.rem(me + 1, count)
    below = lax.rem(me + count - 1, count)
    has_above, has_below = me < count - 1, me > 0
    dev_above = {"chaos": lax.div(above, ncore), "gy": lax.rem(above, ncore)}
    dev_below = {"chaos": lax.div(below, ncore), "gy": lax.rem(below, ncore)}
    dev_right = {"gx": lax.rem(x + 1, ngx)}
    dev_left = {"gx": lax.rem(x + ngx - 1, ngx)}

    def remote(src, dst, ss, rs, dev):
        return pltpu.make_async_remote_copy(
            src_ref=src, dst_ref=dst, send_sem=ss, recv_sem=rs, device_id=dev,
            device_id_type=pl.DeviceIdType.MESH,
        )

    fetch = pltpu.make_async_copy(adj_hbm, adj_ref, in_sem)
    fetch.start()
    barrier = pltpu.get_barrier_semaphore()

    def greet(dev):
        pl.semaphore_signal(barrier, inc=1, device_id=dev, device_id_type=pl.DeviceIdType.MESH)

    for d in range(1, n):
        greet({"chaos": lax.rem(z + d, n)})
    greet(dev_left)
    greet(dev_right)

    greet(dev_above)
    greet(dev_below)
    pl.semaphore_wait(barrier, n + 3)

    def main_copy(to):
        return remote(coef_ref.at[to], kfull.at[z, pl.ds(1, 2)], main_send.at[to], main_recv.at[z], {"chaos": to})

    def v_copies(step, src):
        return (
            remote(src, vhalo.at[step, 0], v_send.at[step, 0], v_recv.at[step, 0], dev_above),
            remote(src, vhalo.at[step, 1], v_send.at[step, 1], v_recv.at[step, 1], dev_below),
            remote(vsend.at[step, 0], vrecv.at[step, 1], v_send.at[step, 2], v_recv.at[step, 2], dev_left),
            remote(vsend.at[step, 1], vrecv.at[step, 0], v_send.at[step, 3], v_recv.at[step, 3], dev_right),
        )

    def start_v(step, src):
        up, down, left, right = v_copies(step, src)

        @pl.when(has_above)
        def _():
            up.start()

        @pl.when(has_below)
        def _():
            down.start()

        for r in range(2):
            flipped = jnp.concatenate([src[r], jnp.zeros((wide - rows_p, 128), f32)], 0).T
            vsend[step, 0, r] = flipped[:8]
            vsend[step, 1, r] = flipped[120:]
        left.start()
        right.start()

    def fwd_copies(j):
        return (
            remote(kfull.at[j, 2], kfull.at[j, 0], fwd_send.at[0, j], fwd_recv.at[0, j], dev_above),
            remote(kfull.at[j, 1], kfull.at[j, 3], fwd_send.at[1, j], fwd_recv.at[1, j], dev_below),
            remote(ksend.at[j, 0], krecv.at[j, 1], fwd_send.at[2, j], fwd_recv.at[2, j], dev_left),
            remote(ksend.at[j, 1], krecv.at[j, 0], fwd_send.at[3, j], fwd_recv.at[3, j], dev_right),
        )

    def forward(j):
        up, down, left, right = fwd_copies(j)

        @pl.when(has_above)
        def _():
            up.start()

        @pl.when(has_below)
        def _():
            down.start()

        for r in range(2):
            flipped = kfull[j, 1 + r].T
            ksend[j, 0, r] = flipped[:8]
            ksend[j, 1, r] = flipped[120:]
        left.start()
        right.start()

    for d in range(1, n):
        main_copy(lax.rem(z + d, n)).start()
    for r in range(2):
        lam_ref[r, :modes] = lam_raw[:, r, :]
        lam_ref[r, modes:] = jnp.zeros((rows_p - modes, 128), f32)
    start_v(0, lam_ref)
    kfull[z, pl.ds(1, 2)] = coef_ref[z]
    forward(z)

    @pl.when(jnp.logical_not(has_below))
    def _():
        kfull[:, 0] = jnp.zeros((n, pts, 128), f32)
        vhalo[:, 0] = jnp.zeros((STEPS, 2, rows_p, 128), f32)

    @pl.when(jnp.logical_not(has_above))
    def _():
        kfull[:, 3] = jnp.zeros((n, pts, 128), f32)
        vhalo[:, 1] = jnp.zeros((STEPS, 2, rows_p, 128), f32)

    lane = lax.broadcasted_iota(jnp.int32, (1, 128), 1)
    quad = quad_ref[...]
    each = jnp.where((quad == 0) | (quad == 3), gauss_weights[0], gauss_weights[1]).astype(f32)
    wts = each[:, :1]
    for d in range(1, inputs):
        wts = wts * each[:, d : d + 1]
    mode_ref[...] = jnp.zeros((16, wide), f32)
    mode_ref[:inputs, :modes] = mode_raw[...].astype(f32)
    wts = wts / jnp.sum(wts, axis=0, keepdims=True) * 0.25
    keep = jnp.where(lax.broadcasted_iota(jnp.int32, (SUB, wide), 1) < modes, 1.0, 0.0).astype(f32)

    def basis(i, carry):
        rows = pl.ds(pl.multiple_of(i * SUB, SUB), SUB)
        q = quad_ref[rows, :]
        node = jnp.where(
            q == 0, gauss_nodes[0], jnp.where(q == 1, gauss_nodes[1], jnp.where(q == 2, gauss_nodes[2], gauss_nodes[3]))
        ).astype(f32)
        h2 = (node * node - 1.0) * (1.0 / math.sqrt(2.0))
        h3 = (node * node * node - 3.0 * node) * (1.0 / math.sqrt(6.0))
        total = keep
        for d in range(inputs):
            deg = mode_ref[d : d + 1, :]
            total = total * jnp.where(
                deg == 0.0,
                1.0,
                jnp.where(deg == 1.0, node[:, d : d + 1], jnp.where(deg == 2.0, h2[:, d : d + 1], h3[:, d : d + 1])),
            )
        psi[rows, :] = total
        high, low = split(total)
        psi_h[rows, :] = high
        psi_l[rows, :] = low
        return carry

    lax.fori_loop(0, points // SUB, basis, 0)
    for i in range(points // 128):
        part = slice(i * 128, i * 128 + 128)
        flipped = (psi[part, :] * wts[part]).T[:rows_p]
        high, low = split(flipped)
        bt_h[:, part] = high
        bt_l[:, part] = low

    def to_points(at, first, second):
        vh, vl = split(jnp.concatenate([first, second], 1))
        res = dot3(psi_h[:, :rows_p], psi_l[:, :rows_p], vh, vl)
        u[at] = res[:, :128]
        u[at + 1] = res[:, 128:]

    def own(src):
        to_points(2, src[0], src[1])

    def sides(step, src):
        left, right = v_copies(step, src)[2:]
        left.wait_recv()
        right.wait_recv()
        edge = [
            jnp.concatenate([vrecv[step, 1, r], jnp.zeros((112, wide), f32), vrecv[step, 0, r]], 0).T[:rows_p]
            for r in range(2)
        ]
        to_points(6, edge[0], edge[1])

    def halo_rows(step, src):
        up, down = v_copies(step, src)[:2]

        @pl.when(has_below)
        def _():
            up.wait_recv()

        to_points(0, vhalo[step, 0, 0], vhalo[step, 0, 1])

        @pl.when(has_above)
        def _():
            down.wait_recv()

        to_points(4, vhalo[step, 1, 0], vhalo[step, 1, 1])

    is_first, is_last = lane == 0, lane == 127

    tile = min(pts, TILE)

    def across(j, i):
        rows = pl.ds(pl.multiple_of(j * pts + i * tile, tile), tile)
        sub = pl.ds(i * tile, tile)
        for r in range(2):
            mid, end = u[2 + r, rows, :], u[6 + r, rows, :]
            a, b = pltpu.roll(mid, 127, 1), pltpu.roll(end, 127, 1)
            e, f = pltpu.roll(mid, 1, 1), pltpu.roll(end, 1, 1)
            fx = kfull[j, 1 + r, sub, :] * (jnp.where(is_last, b, a) - jnp.where(is_first, f, e))
            fe = kedge[j, r, sub, :] * (jnp.where(is_last, a, b) - jnp.where(is_first, e, f))
            nxt = jnp.where(is_last, pltpu.roll(fe, 127, 1), pltpu.roll(fx, 127, 1))
            prv = jnp.where(is_first, pltpu.roll(fe, 1, 1), pltpu.roll(fx, 1, 1))
            d_x[r, rows, :] = nxt - prv

    def along(j, i):
        rows = pl.ds(pl.multiple_of(j * pts + i * tile, tile), tile)
        sub = pl.ds(i * tile, tile)
        uy = [u[k, rows, :] for k in range(6)]
        fy = [kfull[j, k, sub, :] * (uy[k + 2] - uy[k]) for k in range(4)]
        for r in range(2):
            high, low = split(d_x[r, rows, :] + (fy[r + 2] - fy[r]))
            d_h[rows, r * 128 : r * 128 + 128] = high
            d_l[rows, r * 128 : r * 128 + 128] = low

    def chunk(part, j):
        for i in range(pts // tile):
            part(j, i)

    def update(src, store):
        div = dot3(bt_h[...], bt_l[...], d_h[...], d_l[...])
        for r in range(2):
            v = src[r, :modes]
            store(r, v + relax_rate * (adj_ref[:, r, :] - (mass_shift * v - div[:modes, r * 128 : r * 128 + 128])))

    def receive(d):
        j = lax.rem(z + n - d, n)
        remote(coef_ref.at[j], kfull.at[j, pl.ds(1, 2)], main_send.at[j], main_recv.at[j], {"chaos": j}).wait_recv()
        forward(j)

    receive(1)
    third = n // 2

    own(lam_ref)
    for d in range(2, third + 1):
        receive(d)
    sides(0, lam_ref)
    halo_rows(0, lam_ref)
    for d in range(max(2, third + 1), n):
        receive(d)

    def arrive(d, carry):
        j = lax.rem(z + n - d, n)
        up, down, left, right = fwd_copies(j)
        left.wait_recv()
        right.wait_recv()
        for r in range(2):
            kedge[j, r] = jnp.concatenate([krecv[j, 1, r], jnp.zeros((112, pts), f32), krecv[j, 0, r]], 0).T
        chunk(across, j)

        @pl.when(has_below)
        def _():
            up.wait_recv()

        @pl.when(has_above)
        def _():
            down.wait_recv()

        chunk(along, j)
        return carry

    lax.fori_loop(0, n, arrive, 0)

    def keep_lam(r, value):
        lam1[r, :modes] = value
        lam1[r, modes:] = jnp.zeros((rows_p - modes, 128), f32)

    def give(r, value):
        out_ref[:, r, :] = value

    fetch.wait()
    update(lam_ref, keep_lam)
    start_v(1, lam1)
    own(lam1)
    sides(1, lam1)

    def wide_again(j, carry):
        chunk(across, j)
        return carry

    def tall_again(j, carry):
        chunk(along, j)
        return carry

    lax.fori_loop(0, n, wide_again, 0, unroll=n <= 4)
    halo_rows(1, lam1)
    lax.fori_loop(0, n, tall_again, 0, unroll=n <= 4)
    update(lam1, give)

    for d in range(1, n):
        main_copy(lax.rem(z + d, n)).wait_send()

    def drain(copies):
        up, down, left, right = copies

        @pl.when(has_above)
        def _():
            up.wait_send()

        @pl.when(has_below)
        def _():
            down.wait_send()

        left.wait_send()
        right.wait_send()

    def drain_one(j, carry):
        drain(fwd_copies(j))
        return carry

    lax.fori_loop(0, n, drain_one, 0)
    drain(v_copies(0, lam_ref))
    drain(v_copies(1, lam1))


def local(mesh_sizes, lam_start, adj_source, coef_points, quad_index, mode_index):
    n, ngx, ncore = mesh_sizes
    modes = lam_start.shape[0]
    points, inputs = quad_index.shape
    pts = coef_points.shape[0]
    rows_p = -(-modes // 16) * 16
    wide = -(-modes // 128) * 128
    dims = (n, ncore, ngx, inputs, modes, rows_p, wide, points, pts)

    vmem = pl.BlockSpec(memory_space=pltpu.VMEM)
    dma = pltpu.SemaphoreType.DMA
    out = pl.pallas_call(
        functools.partial(kernel, dims),
        out_shape=jax.ShapeDtypeStruct((modes, 2, 128), f32),
        in_specs=[vmem, pl.BlockSpec(memory_space=pltpu.HBM), vmem, vmem, vmem],
        out_specs=vmem,
        scratch_shapes=[
            pltpu.VMEM(lam_start.shape, f32),
            pltpu.SemaphoreType.DMA,
            pltpu.VMEM((2, rows_p, 128), f32),
            pltpu.VMEM((16, wide), f32),
            pltpu.VMEM((n, 4, pts, 128), f32),
            pltpu.VMEM((n, 2, pts, 128), f32),
            pltpu.VMEM((n, 2, 2, 8, pts), f32),
            pltpu.VMEM((n, 2, 2, 8, pts), f32),
            pltpu.VMEM((STEPS, 2, 2, rows_p, 128), f32),
            pltpu.VMEM((STEPS, 2, 2, 8, wide), f32),
            pltpu.VMEM((STEPS, 2, 2, 8, wide), f32),
            pltpu.VMEM((2, rows_p, 128), f32),
            pltpu.VMEM((8, points, 128), f32),
            pltpu.VMEM((points, wide), f32),
            pltpu.VMEM((points, wide), bf16),
            pltpu.VMEM((points, wide), bf16),
            pltpu.VMEM((rows_p, points), bf16),
            pltpu.VMEM((rows_p, points), bf16),
            pltpu.VMEM((points, 256), bf16),
            pltpu.VMEM((points, 256), bf16),
            pltpu.VMEM((2, points, 128), f32),
            dma((n,)), dma((n,)), dma((4, n)), dma((4, n)), dma((STEPS, 4)), dma((STEPS, 4)),
        ],
        compiler_params=pltpu.CompilerParams(
            collective_id=0, has_side_effects=True, vmem_limit_bytes=40 * 1024 * 1024
        ),
    )(lam_start, adj_source, jnp.transpose(coef_points, (1, 2, 0, 3)), quad_index, mode_index.T)
    return out


def solution(mesh):
    sizes = (mesh.shape["chaos"], mesh.shape["gx"], mesh.shape["gy"])
    placed = (
        P(None, ("chaos", "gy"), "gx"),
        P(None, ("chaos", "gy"), "gx"),
        P("chaos", None, "gy", "gx"),
        P(),
        P(),
    )
    return jax.shard_map(
        functools.partial(local, sizes),
        mesh=mesh,
        in_specs=placed,
        out_specs=P(None, ("chaos", "gy"), "gx"),
        check_vma=False,
    )
```
